32 devices in a mesh: batch: 4 (over z), seq: 8 (over y, x, core).
Axes of the slice: x: 2, y: 2, z: 4, core: 2. Of those that a mesh axis runs over, the one named last changes fastest.
Arguments:
- inputs: bfloat16 [2, 4, 4096, 768], P(None, 'batch', 'seq'), may hold values from -6 to 6
- cotangent: bfloat16 [2, 4, 4096, 768], P(None, 'batch', 'seq'), may hold values from -6 to 6
- pre_gain: bfloat16 [768], P(('batch', 'seq')), may hold values from 0.099609375 to 1.8984375
- qkv_weight: bfloat16 [768, 2304], P(('batch', 'seq')), may hold values from -0.21875 to 0.21875
- qv_bias: bfloat16 [1536], P(('batch', 'seq')), may hold values from -3 to 3
- mid_gain: bfloat16 [768], P(('batch', 'seq')), may hold values from 0.099609375 to 1.8984375
- out_weight: bfloat16 [768, 768], P(('batch', 'seq')), may hold values from -0.21875 to 0.21875
- out_bias: bfloat16 [768], P(('batch', 'seq')), may hold values from -3 to 3
- ffn_gain: bfloat16 [768], P(('batch', 'seq')), may hold values from 0.099609375 to 1.8984375
- up_weight: bfloat16 [768, 3072], P(('batch', 'seq')), may hold values from -0.21875 to 0.21875
- up_bias: bfloat16 [3072], P(('batch', 'seq')), may hold values from -3 to 3
- sub_gain: bfloat16 [3072], P(('batch', 'seq')), may hold values from 0.099609375 to 1.8984375
- down_weight: bfloat16 [3072, 768], P(('batch', 'seq')), may hold values from -0.109375 to 0.109375
- down_bias: bfloat16 [768], P(('batch', 'seq')), may hold values from -3 to 3
- pic_starts: int32 [2, 4, 4], P(None, 'batch'), may hold values from 0 to 3840, as said below
- head_offsets: int32 [12], replicated, may hold values from 0 to 1
Outputs:
- layer_out: bfloat16 [2, 4, 4096, 768], P(None, 'batch', 'seq')
- input_grad: bfloat16 [2, 4, 4096, 768], P(None, 'batch', 'seq')
- pregain_grad: float32 [768], P(('batch', 'seq'))
- qkv_grad: float32 [768, 2304], P(('batch', 'seq'))
- qvbias_grad: float32 [1536], P(('batch', 'seq'))
- midgain_grad: float32 [768], P(('batch', 'seq'))
- outweight_grad: float32 [768, 768], P(('batch', 'seq'))
- outbias_grad: float32 [768], P(('batch', 'seq'))
- ffngain_grad: float32 [768], P(('batch', 'seq'))
- upweight_grad: float32 [768, 3072], P(('batch', 'seq'))
- upbias_grad: float32 [3072], P(('batch', 'seq'))
- subgain_grad: float32 [3072], P(('batch', 'seq'))
- downweight_grad: float32 [3072, 768], P(('batch', 'seq'))
- downbias_grad: float32 [768], P(('batch', 'seq'))
The draws below stay inside these ranges and needn't reach their ends.
Inputs may be any that keep to these rules, and one draw needn't show every extreme that they name: `pic_starts`: piece n of a sequence starts at n * 1024 or later and ends by (n + 1) * 1024, so pieces never intersect.
All inputs are finite; a program needn't handle non-finite values.
Results may differ from the reference program's by a relative error of at most 0.019.
Values may be sent and summed in bfloat16 or wider, within the bound.
No kernel may reach another device: no remote copies, remote signals or barrier semaphores. Data moves between devices by JAX's collectives and lax.ppermute only.
A program may use at most 384 MiB of HBM per device.

```python
import math
import jax
import jax.numpy as jnp
from jax import lax

D = 768
HEADS = 12
HD = 64
FF = 3072
MICRO = 2
LEN = 4096
SEG_SHORT = 2048
SEG_LONG = 4096
PIC = 256
NPIC = 4
NS_ALL = 4
L_LOC = 512
N_SEQ = 8


def draw_pic_starts(key, part):
    region = LEN // NPIC
    shifted = jax.random.randint(key, (MICRO, NS_ALL, NPIC), 0, region - PIC + 1, dtype=jnp.int32)
    return shifted + jnp.arange(NPIC, dtype=jnp.int32) * region


def set_ends(entries, key, smallest, high):
    shape = entries.shape
    spot = [jax.random.randint(jax.random.fold_in(key, axis), (), 0, shape[axis]) for axis in range(len(shape))]
    entries = entries.at[tuple(spot)].set(smallest)
    longest = shape.index(max(shape))
    spot[longest] = (spot[longest] + 1) % shape[longest]
    return entries.at[tuple(spot)].set(high)


def steps_of(key, shape, cuts, least, top_value):
    def one(position, blocks):
        heights = jax.random.uniform(jax.random.fold_in(jax.random.fold_in(key, 6), position), (blocks,), jnp.float32, least / len(cuts), top_value / len(cuts))
        return jnp.repeat(jnp.exp(heights), shape[position] // blocks).reshape((-1,) + (1,) * (len(shape) - position - 1))

    level = one(*cuts[0])
    for cut in cuts[1:]:
        level = level * one(*cut)
    return level


def noise(key, extent, deviation, bound, cuts=(), kind=jnp.bfloat16):
    values = jax.random.normal(key, extent, jnp.float32) * deviation
    if len(cuts) > 0:
        values = steps_of(key, extent, cuts, -0.22, 0.18) * values
    return jnp.clip(values, min=-bound, max=bound).astype(kind)


def setup_inputs(seed: int = 0) -> dict:
    key_of = jax.random.split(jax.random.key(seed), 17)
    inputs = noise(key_of[0], (MICRO, NS_ALL, LEN, D), 1.0, 6.0, ((1, 4), (2, 8)))
    cotangent = noise(key_of[1], (MICRO, NS_ALL, LEN, D), 1.0, 6.0, ((1, 4), (2, 8)))
    pre_gain = jnp.clip(1.0 + 0.18 * jax.random.normal(key_of[2], (D,), jnp.float32), 0.099609375, 1.8984375).astype(jnp.bfloat16)
    qkv_weight = noise(key_of[3], (D, 3 * D), D ** -0.5, 0.21875, ((0, 32),))
    qv_bias = noise(key_of[4], (2 * D,), 0.5, 3.0, ((0, 32),))
    mid_gain = jnp.clip(1.0 + 0.18 * jax.random.normal(key_of[5], (D,), jnp.float32), 0.099609375, 1.8984375).astype(jnp.bfloat16)
    out_weight = noise(key_of[6], (D, D), D ** -0.5, 0.21875, ((0, 32),))
    out_bias = noise(key_of[7], (D,), 0.5, 3.0, ((0, 32),))
    ffn_gain = jnp.clip(1.0 + 0.18 * jax.random.normal(key_of[8], (D,), jnp.float32), 0.099609375, 1.8984375).astype(jnp.bfloat16)
    up_weight = noise(key_of[9], (D, FF), D ** -0.5, 0.21875, ((0, 32),))
    up_bias = noise(key_of[10], (FF,), 0.5, 3.0, ((0, 32),))
    sub_gain = jnp.clip(1.0 + 0.18 * jax.random.normal(key_of[11], (FF,), jnp.float32), 0.099609375, 1.8984375).astype(jnp.bfloat16)
    down_weight = noise(key_of[12], (FF, D), FF ** -0.5, 0.109375, ((0, 32),))
    down_bias = noise(key_of[13], (D,), 0.5, 3.0, ((0, 32),))
    pic_starts = draw_pic_starts(jax.random.fold_in(key_of[16], 71), 0)
    head_offsets = set_ends(jax.random.randint(key_of[15], (HEADS,), 0, 2), jax.random.fold_in(key_of[15], 1), 0, 1).astype(jnp.int32)
    return {"inputs": inputs, "cotangent": cotangent, "pre_gain": pre_gain, "qkv_weight": qkv_weight, "qv_bias": qv_bias, "mid_gain": mid_gain, "out_weight": out_weight, "out_bias": out_bias, "ffn_gain": ffn_gain, "up_weight": up_weight, "up_bias": up_bias, "sub_gain": sub_gain, "down_weight": down_weight, "down_bias": down_bias, "pic_starts": pic_starts, "head_offsets": head_offsets}


@jax.custom_vjp
def low(v):
    return lax.optimization_barrier(v.astype(jnp.bfloat16)).astype(jnp.float32)

@jax.custom_vjp
def low_back(v):
    return v

def low_keep(v):
    return (low(v), None)

def low_pass(kept, grad):
    return (grad,)

def back_keep(v):
    return (v, None)

def back_low(kept, grad):
    return (low(grad),)
low.defvjp(low_keep, low_pass)
low_back.defvjp(back_keep, back_low)

def layer_norm(values, gain):
    centred = values - lax.optimization_barrier(jnp.mean(values, axis=-1, keepdims=True))
    spread = lax.optimization_barrier(jnp.mean(centred * centred, axis=-1, keepdims=True))
    return centred * lax.rsqrt(spread + 1e-05) * gain

def piece_table(positions, starts):
    inside = (positions[None, :, None] >= starts[:, None, :]) & (positions[None, :, None] < starts[:, None, :] + PIC)
    labels = jnp.arange(1, starts.shape[1] + 1, dtype=jnp.int32)
    return lax.optimization_barrier(jnp.sum(jnp.where(inside, labels, 0), axis=-1))

def multiplicity(query_pos, key_pos, starts, offsets):
    query_piece = piece_table(query_pos, starts)
    key_piece = piece_table(key_pos, starts)
    shared = (key_piece.T[:, :, None] == query_piece[None, :, :]) & (query_piece[None, :, :] > 0)
    causal = (key_pos[:, None] <= query_pos[None, :])[:, None, :]
    allowed = shared | causal
    key_col = key_pos[:, None]
    query_row = query_pos[None, :]
    near_segment = (key_col // SEG_SHORT == query_row // SEG_SHORT)[:, None, :]
    far_segment = ((key_col // SEG_LONG == query_row // SEG_LONG) & (key_col % 2 == query_row % 2))[:, None, :]
    active = query_row % 2 == offsets[:, None]
    first_count = (allowed & near_segment).astype(jnp.float32)[:, :, None, :]
    second = ((allowed & far_segment)[:, :, None, :] & active[None, None, :, :]).astype(jnp.float32)
    return first_count + second

def attend_rows(queries, key_values, query_pos, starts, offsets):
    rounded_pairs = low_back(key_values)
    key_rows = rounded_pairs[:, :D].reshape(LEN, HEADS, HD)
    values = rounded_pairs[:, D:].reshape(LEN, HEADS, HD)
    key_pos = jnp.arange(LEN, dtype=jnp.int32)
    score_scale = 1.0 / math.sqrt(HD)
    scores = low_back(jnp.einsum('qhe,khe->khq', queries, key_rows, precision=lax.Precision.HIGHEST) * score_scale)
    counts = multiplicity(query_pos, key_pos, starts[None, :], offsets)[:, 0]
    running_max = lax.optimization_barrier(jnp.max(jnp.where(counts > 0, scores, -1e+30), axis=0))
    running_sum = lax.optimization_barrier(jnp.sum(counts * jnp.exp(jnp.where(counts > 0, scores - running_max, -1e+30)), axis=0))
    log_total = running_max + jnp.log(running_sum)
    weights = low(counts * jnp.exp(jnp.where(counts > 0, scores - log_total, -1e+30)))
    return jnp.einsum('khq,khe->qhe', weights, values, precision=lax.Precision.HIGHEST)

def layer(tokens_in, params, starts, offsets):
    gain_pre, weight_qkv, bias_qv, gain_mid, weight_out, bias_out, gain_ffn, weight_up, bias_up, gain_sub, weight_down, bias_down = params
    high = lax.Precision.HIGHEST
    normed = low(layer_norm(tokens_in, gain_pre))
    bias_full = jnp.concatenate([bias_qv[:D], jnp.zeros((D,), tokens_in.dtype), bias_qv[D:]])
    projected = low_back(low(jnp.dot(normed, weight_qkv, precision=high) + bias_full))
    queries = projected[:, :D].reshape(N_SEQ, L_LOC, HEADS, HD)
    key_values = projected[:, D:]
    positions = jnp.arange(LEN, dtype=jnp.int32).reshape(N_SEQ, L_LOC)

    def one_block(item):
        return attend_rows(item[0], key_values, item[1], starts, offsets)
    attended = lax.map(jax.checkpoint(one_block), (queries, positions)).reshape(LEN, D)
    attended = low_back(attended)
    mid_normed = low(layer_norm(attended, gain_mid))
    middle = tokens_in + low_back(jnp.dot(mid_normed, weight_out, precision=high) + bias_out)
    ffn_normed = low(layer_norm(middle, gain_ffn))
    before = low_back(jnp.dot(ffn_normed, weight_up, precision=high) + bias_up)
    activated = jax.nn.gelu(before, approximate=False)
    sub_normed = low(layer_norm(activated, gain_sub))
    return middle + low_back(jnp.dot(sub_normed, weight_down, precision=high) + bias_down)

def reference(inputs, cotangent, pre_gain, qkv_weight, qv_bias, mid_gain, out_weight, out_bias, ffn_gain, up_weight, up_bias, sub_gain, down_weight, down_bias, pic_starts, head_offsets):
    params = tuple((item.astype(jnp.float32) for item in (pre_gain, qkv_weight, qv_bias, mid_gain, out_weight, out_bias, ffn_gain, up_weight, up_bias, sub_gain, down_weight, down_bias)))
    sequences = MICRO * NS_ALL
    flat_in = inputs.reshape(sequences, LEN, D)
    flat_cot = cotangent.reshape(sequences, LEN, D)
    flat_starts = pic_starts.reshape(sequences, NPIC).astype(jnp.int32)

    def one_sequence(carry, item):
        tokens, upstream, starts = item

        def run(tokens_in, *weights):
            return layer(tokens_in, weights, starts, head_offsets)
        result, back = jax.vjp(run, tokens.astype(jnp.float32), *params)
        grads = back(upstream.astype(jnp.float32))
        carry = tuple((first + second for first, second in zip(carry, grads[1:])))
        return (carry, (result.astype(jnp.bfloat16), grads[0].astype(jnp.bfloat16)))
    initial = tuple((jnp.zeros_like(item) for item in params))
    sums, (outputs, input_grads) = lax.scan(one_sequence, initial, (flat_in, flat_cot, flat_starts))
    return (outputs.reshape(inputs.shape), input_grads.reshape(inputs.shape), sums[0], sums[1], sums[2], sums[3], sums[4], sums[5], sums[6], sums[7], sums[8], sums[9], sums[10], sums[11])
```

```python
import math

import jax
import jax.numpy as jnp
import numpy as np
from jax import lax
from jax.experimental import pallas as pl
from jax.experimental.pallas import tpu as pltpu
from jax.sharding import Mesh
from jax.sharding import PartitionSpec as P

HEADS = 12
HD = 64
SEG = 2048
PIC = 256
HALF = SEG // 2
TILE = 256
NT = HALF // TILE
NEG = -1e30
EXP_SCALE = math.log2(math.e) / math.sqrt(HD)
SCORE_SCALE = 1.0 / math.sqrt(HD)
ALL = ("batch", "seg", "grp", "core")
F32 = jnp.float32
BF16 = jnp.bfloat16


def dot(a, b, ca, cb):
    return lax.dot_general(a, b, (((ca,), (cb,)), ((), ())), preferred_element_type=F32)


def class_base(off, number):
    parity = off if number == 0 else 1 - off
    return parity * HALF


def masked(scores, limit_row, first_key):
    keys = 2 * lax.broadcasted_iota(jnp.int32, scores.shape, 0)
    return jnp.where(keys <= limit_row - first_key, scores, NEG)


def softmax_step(state, queries, keys, values_t, shift, limit_row=None, first_key=None):
    top, total, acc = state
    scores = dot(keys, queries, 1, 0) * EXP_SCALE
    if limit_row is not None:
        scores = masked(scores, limit_row, first_key)
    new_top = jnp.maximum(top, jnp.max(scores, axis=0, keepdims=True))
    factor = jnp.exp2(top - new_top)
    weights = jnp.exp2(scores - (new_top - shift))
    total = total * factor + jnp.sum(weights, axis=0, keepdims=True)
    acc = acc * factor + dot(values_t, weights.astype(BF16), 1, 0)
    return (new_top, total, acc)


def near_forward_kernel(off_ref, flag_ref, lim_ref, q_ref, k_ref, v_ref, acc_ref, stat_ref, key_ref):
    pair = pl.program_id(0)
    for h in range(2):
        for c in range(SEG // 512):
            cols = pl.ds(c * 512, 512)
            key_ref[h, cols, :] = k_ref[h * HD : (h + 1) * HD, cols].T

    def per_tile(t, carry):
        cls = t // NT
        i = t % NT
        first = jnp.where(cls == 0, 1.0, 0.0).astype(F32)
        heads = []
        for h in range(2):
            off = off_ref[pair * 2 + h]
            own = jnp.where(cls == 0, off, 1 - off)
            base = pl.multiple_of(own * HALF + i * TILE, TILE)
            queries = q_ref[h * HD : (h + 1) * HD, pl.ds(base, TILE)]
            heads.append((off, base, queries, lim_ref[:, pl.ds(base, TILE)]))

        def step(states, other, j, use_mask):
            out = []
            for h in range(2):
                off, base, queries, limit_row = heads[h]
                parity = off if other == 0 else 1 - off
                start = pl.multiple_of(parity * HALF + j * TILE, TILE)
                keys = key_ref[h, pl.ds(start, TILE), :]
                values_t = v_ref[h * HD : (h + 1) * HD, pl.ds(start, TILE)]
                shift = first if other == 0 else 0.0
                if use_mask:
                    out.append(
                        softmax_step(
                            states[h], queries, keys, values_t, shift, limit_row, 2 * TILE * j + parity
                        )
                    )
                else:
                    out.append(softmax_step(states[h], queries, keys, values_t, shift))
            return tuple(out)

        initial = (
            jnp.full((1, TILE), NEG, F32),
            jnp.zeros((1, TILE), F32),
            jnp.zeros((HD, TILE), F32),
        )
        states = (initial, initial)
        extra = jnp.logical_and(i % 2 == 0, flag_ref[i // 2] > 0)
        for other in range(2):
            states = lax.fori_loop(0, i, lambda j, s, o=other: step(s, o, j, False), states)
            states = step(states, other, i, True)
            states = lax.cond(
                extra, lambda s, o=other: step(s, o, i + 1, True), lambda s: s, states
            )
        for h in range(2):
            base = heads[h][1]
            top, total, acc = states[h]
            acc_ref[h * HD : (h + 1) * HD, pl.ds(base, TILE)] = acc
            stat_ref[0, h : h + 1, pl.ds(base, TILE)] = top
            stat_ref[0, 2 + h : 3 + h, pl.ds(base, TILE)] = total
        return carry

    lax.fori_loop(0, 2 * NT, per_tile, 0)


def far_forward_kernel(
    off_ref, far_ref, q_ref, kx_ref, vx_ref, acc_in, stat_in, o_ref, lse_ref, key_ref
):
    pair = pl.program_id(0)
    for h in range(2):
        for c in range(HALF // 512):
            cols = pl.ds(c * 512, 512)
            key_ref[h, cols, :] = kx_ref[h * HD : (h + 1) * HD, cols].T

    def per_tile(i, carry):
        bases = []
        states = []
        for h in range(2):
            off = off_ref[pair * 2 + h]
            base = pl.multiple_of(off * HALF + i * TILE, TILE)
            rest = pl.multiple_of((1 - off) * HALF + i * TILE, TILE)
            bases.append((base, rest))
            cols = pl.ds(base, TILE)
            states.append(
                (
                    stat_in[0, h : h + 1, cols],
                    stat_in[0, 2 + h : 3 + h, cols],
                    acc_in[h * HD : (h + 1) * HD, cols],
                )
            )

        def step(j, now):
            out = []
            for h in range(2):
                start = pl.multiple_of(j * TILE, TILE)
                out.append(
                    softmax_step(
                        now[h],
                        q_ref[h * HD : (h + 1) * HD, pl.ds(bases[h][0], TILE)],
                        key_ref[h, pl.ds(start, TILE), :],
                        vx_ref[h * HD : (h + 1) * HD, pl.ds(start, TILE)],
                        0.0,
                    )
                )
            return tuple(out)

        states = lax.fori_loop(0, far_ref[0] * NT, step, tuple(states))
        for h in range(2):
            base, rest = bases[h]
            rows = slice(h * HD, (h + 1) * HD)
            top, total, acc = states[h]
            o_ref[rows, pl.ds(base, TILE)] = acc / total
            lse_ref[0, h : h + 1, pl.ds(base, TILE)] = top + jnp.log2(total)
            cols = pl.ds(rest, TILE)
            top = stat_in[0, h : h + 1, cols]
            total = stat_in[0, 2 + h : 3 + h, cols]
            o_ref[rows, cols] = acc_in[rows, cols] / total
            lse_ref[0, h : h + 1, cols] = top + jnp.log2(total)
        return carry

    lax.fori_loop(0, NT, per_tile, 0)


def slopes_step(queries, keys, values, grads, lse_row, dot_row, limit_row=None, first_key=None):
    scores = dot(keys, queries, 1, 0) * EXP_SCALE
    if limit_row is not None:
        scores = masked(scores, limit_row, first_key)
    probs = jnp.exp2(scores - lse_row)
    inner = dot(values, grads, 1, 0)
    slopes = (probs * (inner - dot_row)).astype(BF16)
    return probs.astype(BF16), slopes


def far_backward_kernel(
    off_ref,
    far_ref,
    q_ref,
    kx_ref,
    vx_ref,
    g_ref,
    o_ref,
    lse_ref,
    dq_ref,
    dkv_ref,
    key_ref,
    val_ref,
):
    pair = pl.program_id(0)

    @pl.when(far_ref[0] == 0)
    def _():
        dq_ref[...] = jnp.zeros_like(dq_ref)
        dkv_ref[...] = jnp.zeros_like(dkv_ref)

    @pl.when(far_ref[0] > 0)
    def _():
        for h in range(2):
            rows = slice(h * HD, (h + 1) * HD)
            for c in range(HALF // 512):
                cols = pl.ds(c * 512, 512)
                key_ref[h, cols, :] = kx_ref[rows, cols].T
                val_ref[h, cols, :] = vx_ref[rows, cols].T
        dq_ref[...] = jnp.zeros_like(dq_ref)

        def per_tile(j, carry):
            start = pl.multiple_of(j * TILE, TILE)
            kcols = pl.ds(start, TILE)

            def step(i, sums):
                out = []
                for h in range(2):
                    rows = slice(h * HD, (h + 1) * HD)
                    off = off_ref[pair * 2 + h]
                    qcols = pl.ds(pl.multiple_of(off * HALF + i * TILE, TILE), TILE)
                    queries = q_ref[rows, qcols]
                    grads = g_ref[rows, qcols]
                    dot_row = jnp.sum(grads.astype(F32) * o_ref[rows, qcols], axis=0, keepdims=True)
                    probs, slopes = slopes_step(
                        queries,
                        key_ref[h, kcols, :],
                        val_ref[h, kcols, :],
                        grads,
                        lse_ref[0, h : h + 1, qcols],
                        dot_row,
                    )
                    dk, dv = sums[h]
                    dk = dk + dot(queries, slopes, 1, 1)
                    dv = dv + dot(grads, probs, 1, 1)
                    out.append((dk, dv))
                    here = pl.ds(pl.multiple_of(i * TILE, TILE), TILE)
                    dq_ref[rows, here] += dot(kx_ref[rows, kcols], slopes, 1, 0)
                return tuple(out)

            zero = jnp.zeros((HD, TILE), F32)
            sums = lax.fori_loop(0, NT, step, ((zero, zero), (zero, zero)))
            for h in range(2):
                rows = slice(h * HD, (h + 1) * HD)
                dkv_ref[0, rows, kcols] = (sums[h][0] * SCORE_SCALE).astype(BF16)
                dkv_ref[1, rows, kcols] = sums[h][1].astype(BF16)
            return carry

        lax.fori_loop(0, NT, per_tile, 0)


def near_backward_kernel(
    off_ref,
    flag_ref,
    lim_ref,
    q_ref,
    k_ref,
    v_ref,
    g_ref,
    o_ref,
    lse_ref,
    dqx_ref,
    out_ref,
    key_ref,
    val_ref,
    dq_ref,
    row_ref,
):
    pair = pl.program_id(0)
    for h in range(2):
        rows = slice(h * HD, (h + 1) * HD)
        off = off_ref[pair * 2 + h]
        for c in range(SEG // 512):
            cols = pl.ds(c * 512, 512)
            key_ref[h, cols, :] = k_ref[rows, cols].T
            val_ref[h, cols, :] = v_ref[rows, cols].T
            row_ref[h : h + 1, cols] = jnp.sum(
                g_ref[rows, cols].astype(F32) * o_ref[rows, cols], axis=0, keepdims=True
            )
        active = pl.ds(pl.multiple_of(off * HALF, HALF), HALF)
        rest = pl.ds(pl.multiple_of((1 - off) * HALF, HALF), HALF)
        dq_ref[rows, active] = dqx_ref[rows, :]
        dq_ref[rows, rest] = jnp.zeros((HD, HALF), F32)

    def per_tile(t, carry):
        cls = t // NT
        j = t % NT
        first = jnp.where(cls == 0, 1.0, 0.0).astype(F32)
        starts = []
        for h in range(2):
            off = off_ref[pair * 2 + h]
            parity = jnp.where(cls == 0, off, 1 - off)
            starts.append((parity, pl.multiple_of(parity * HALF + j * TILE, TILE)))

        def step(sums, other, i, use_mask):
            out = []
            for h in range(2):
                rows = slice(h * HD, (h + 1) * HD)
                off = off_ref[pair * 2 + h]
                own = off if other == 0 else 1 - off
                qcols = pl.ds(pl.multiple_of(own * HALF + i * TILE, TILE), TILE)
                parity, start = starts[h]
                kcols = pl.ds(start, TILE)
                queries = q_ref[rows, qcols]
                grads = g_ref[rows, qcols]
                lse_row = lse_ref[0, h : h + 1, qcols]
                if other == 0:
                    lse_row = lse_row - first
                extra = (lim_ref[:, qcols], 2 * TILE * j + parity) if use_mask else ()
                probs, slopes = slopes_step(
                    queries,
                    key_ref[h, kcols, :],
                    val_ref[h, kcols, :],
                    grads,
                    lse_row,
                    row_ref[h : h + 1, qcols],
                    *extra,
                )
                dk, dv = sums[h]
                dk = dk + dot(queries, slopes, 1, 1)
                dv = dv + dot(grads, probs, 1, 1)
                out.append((dk, dv))
                dq_ref[rows, qcols] += dot(k_ref[rows, kcols], slopes, 1, 0)
            return tuple(out)

        zero = jnp.zeros((HD, TILE), F32)
        sums = ((zero, zero), (zero, zero))
        extra = jnp.logical_and(j % 2 == 1, flag_ref[j // 2] > 0)
        for other in range(2):
            sums = step(sums, other, j, True)
            sums = lax.cond(extra, lambda s, o=other: step(s, o, j - 1, True), lambda s: s, sums)
            sums = lax.fori_loop(j + 1, NT, lambda i, s, o=other: step(s, o, i, False), sums)
        for h in range(2):
            rows = slice(h * HD, (h + 1) * HD)
            kcols = pl.ds(starts[h][1], TILE)
            out_ref[1, rows, kcols] = (sums[h][0] * SCORE_SCALE).astype(BF16)
            out_ref[2, rows, kcols] = sums[h][1].astype(BF16)
        return carry

    lax.fori_loop(0, 2 * NT, per_tile, 0)
    out_ref[0] = (dq_ref[...] * SCORE_SCALE).astype(BF16)


def smem():
    return pl.BlockSpec(memory_space=pltpu.SMEM)


def rows_spec(first, width=SEG):
    return pl.BlockSpec((2 * HD, width), lambda p, f=first: (f + p, 0))


def stat_spec():
    return pl.BlockSpec((1, 8, SEG), lambda p: (p, 0, 0))


def near_forward(offsets, flags, limits, proj_t):
    pairs = offsets.shape[0] // 2
    return pl.pallas_call(
        near_forward_kernel,
        grid=(pairs,),
        in_specs=[
            smem(),
            smem(),
            pl.BlockSpec((1, SEG), lambda p: (0, 0)),
            rows_spec(0),
            rows_spec(pairs),
            rows_spec(2 * pairs),
        ],
        out_specs=[rows_spec(0), stat_spec()],
        out_shape=[
            jax.ShapeDtypeStruct((pairs * 2 * HD, SEG), F32),
            jax.ShapeDtypeStruct((pairs, 8, SEG), F32),
        ],
        scratch_shapes=[pltpu.VMEM((2, SEG, HD), BF16)],
        cost_estimate=pl.CostEstimate(
            flops=pairs * 4 * SEG * SEG * HD * 2, transcendentals=pairs * SEG * SEG, bytes_accessed=8 << 20
        ),
        name="near_forward",
    )(offsets, flags, limits, proj_t, proj_t, proj_t)


def far_forward(offsets, far, proj_t, pair_t, acc, stats):
    pairs = offsets.shape[0] // 2
    return pl.pallas_call(
        far_forward_kernel,
        grid=(pairs,),
        in_specs=[
            smem(),
            smem(),
            rows_spec(0),
            rows_spec(0, HALF),
            rows_spec(pairs, HALF),
            rows_spec(0),
            stat_spec(),
        ],
        out_specs=[rows_spec(0), stat_spec()],
        out_shape=[
            jax.ShapeDtypeStruct((pairs * 2 * HD, SEG), F32),
            jax.ShapeDtypeStruct((pairs, 8, SEG), F32),
        ],
        scratch_shapes=[pltpu.VMEM((2, HALF, HD), BF16)],
        cost_estimate=pl.CostEstimate(
            flops=pairs * 2 * SEG * SEG * HD, transcendentals=pairs * HALF * SEG, bytes_accessed=8 << 20
        ),
        name="far_forward",
    )(offsets, far, proj_t, pair_t, pair_t, acc, stats)


def far_backward(offsets, far, proj_t, pair_t, grads_t, out_t, lse):
    pairs = offsets.shape[0] // 2
    return pl.pallas_call(
        far_backward_kernel,
        grid=(pairs,),
        in_specs=[
            smem(),
            smem(),
            rows_spec(0),
            rows_spec(0, HALF),
            rows_spec(pairs, HALF),
            rows_spec(0),
            rows_spec(0),
            stat_spec(),
        ],
        out_specs=[
            rows_spec(0, HALF),
            pl.BlockSpec((2, 2 * HD, HALF), lambda p: (0, p, 0)),
        ],
        out_shape=[
            jax.ShapeDtypeStruct((pairs * 2 * HD, HALF), F32),
            jax.ShapeDtypeStruct((2, pairs * 2 * HD, HALF), BF16),
        ],
        scratch_shapes=[pltpu.VMEM((2, HALF, HD), BF16), pltpu.VMEM((2, HALF, HD), BF16)],
        cost_estimate=pl.CostEstimate(
            flops=pairs * 5 * SEG * SEG * HD, transcendentals=pairs * HALF * SEG, bytes_accessed=10 << 20
        ),
        name="far_backward",
    )(offsets, far, proj_t, pair_t, pair_t, grads_t, out_t, lse)


def near_backward(offsets, flags, limits, proj_t, grads_t, out_t, lse, dq_far):
    pairs = offsets.shape[0] // 2
    return pl.pallas_call(
        near_backward_kernel,
        grid=(pairs,),
        in_specs=[
            smem(),
            smem(),
            pl.BlockSpec((1, SEG), lambda p: (0, 0)),
            rows_spec(0),
            rows_spec(pairs),
            rows_spec(2 * pairs),
            rows_spec(0),
            rows_spec(0),
            stat_spec(),
            rows_spec(0, HALF),
        ],
        out_specs=pl.BlockSpec((3, 2 * HD, SEG), lambda p: (0, p, 0)),
        out_shape=jax.ShapeDtypeStruct((3, pairs * 2 * HD, SEG), BF16),
        scratch_shapes=[
            pltpu.VMEM((2, SEG, HD), BF16),
            pltpu.VMEM((2, SEG, HD), BF16),
            pltpu.VMEM((2 * HD, SEG), F32),
            pltpu.VMEM((8, SEG), F32),
        ],
        cost_estimate=pl.CostEstimate(
            flops=pairs * 10 * SEG * SEG * HD * 2, transcendentals=pairs * SEG * SEG, bytes_accessed=14 << 20
        ),
        name="near_backward",
    )(offsets, flags, limits, proj_t, proj_t, proj_t, grads_t, out_t, lse, dq_far)


def normalize(values):
    centred = values - jnp.mean(values, axis=-1, keepdims=True)
    spread = jnp.mean(centred * centred, axis=-1, keepdims=True)
    scale = lax.rsqrt(spread + 1e-05)
    return centred * scale, scale


def norm_back(unit, scale, gain, grad):
    scaled = grad * gain
    first = jnp.mean(scaled, axis=-1, keepdims=True)
    second = jnp.mean(scaled * unit, axis=-1, keepdims=True)
    values = (scaled - first - unit * second) * scale
    return values, jnp.sum(grad * unit, axis=0)


def gelu_and_slope(u):
    cdf = 0.5 * (1.0 + lax.erf(u * math.sqrt(0.5)))
    density = jnp.exp(-0.5 * u * u) * (1.0 / math.sqrt(2.0 * math.pi))
    return u * cdf, cdf + u * density


def flip(values, axis):
    return lax.ppermute(values, axis, [(0, 1), (1, 0)])


def spread_items(items):
    groups = lax.axis_size("grp")
    if groups != 2:
        return lax.all_to_all(items, "grp", 0, 0, tiled=True)
    me = lax.axis_index("grp")
    mine = lax.dynamic_index_in_dim(items, me, 0, keepdims=False)
    other = flip(lax.dynamic_index_in_dim(items, 1 - me, 0, keepdims=False), "grp")
    swap = me == 1
    return jnp.stack([jnp.where(swap, other, mine), jnp.where(swap, mine, other)])


def on_device(
    inputs,
    cotangent,
    pre_gain,
    qkv_weight,
    qv_bias,
    mid_gain,
    out_weight,
    out_bias,
    ffn_gain,
    up_weight,
    up_bias,
    sub_gain,
    down_weight,
    down_bias,
    pic_starts,
    head_offsets,
):
    micro, sequences, local, width = inputs.shape
    groups = lax.axis_size("grp")
    items = micro * sequences
    half = local // 2
    own_rows = groups * local
    core_heads = HEADS // 2
    core_width = core_heads * HD
    seg = lax.axis_index("seg")
    grp = lax.axis_index("grp")
    core = lax.axis_index("core")

    order = np.concatenate([np.arange(0, local, 2), np.arange(1, local, 2)])
    split = np.zeros((local, local), np.float32)
    split[np.arange(local), order] = 1.0
    split = jnp.asarray(split, BF16)

    def arrange(tokens):
        tokens = tokens.reshape(items, local, width)
        tokens = jnp.einsum("rs,isd->ird", split, tokens, preferred_element_type=F32).astype(BF16)
        tokens = spread_items(tokens)
        return tokens.reshape(groups, 2, half, width).transpose(1, 0, 2, 3)

    def restore(tokens):
        tokens = tokens.reshape(2, groups, half, width).transpose(1, 0, 2, 3)
        tokens = spread_items(tokens.reshape(groups, local, width))
        tokens = jnp.einsum("rs,ird->isd", split, tokens, preferred_element_type=F32).astype(BF16)
        return tokens.reshape(inputs.shape)

    def join_cores(own, theirs, axis):
        swap = core == 1
        return jnp.stack([jnp.where(swap, theirs, own), jnp.where(swap, own, theirs)], axis=axis)

    def gather(shard):
        return lax.all_gather(shard, ALL, axis=0, tiled=True)

    small = jnp.concatenate(
        [pre_gain, qv_bias, mid_gain, out_bias, ffn_gain, up_bias, sub_gain, down_bias]
    )
    small_all = lax.all_gather(small, ALL, axis=0).astype(F32)
    sizes = [v.shape[0] for v in (pre_gain, qv_bias, mid_gain, out_bias, ffn_gain, up_bias, sub_gain, down_bias)]
    parts = []
    at = 0
    for size in sizes:
        parts.append(small_all[:, at : at + size].reshape(-1))
        at += size
    gain_pre, bias_qv, gain_mid, bias_out, gain_ffn, bias_up, gain_sub, bias_down = parts

    weight_qkv = gather(qkv_weight).reshape(width, 3, 2, core_width)
    weight_core = lax.dynamic_index_in_dim(weight_qkv, core, 2, keepdims=False)
    weight_core = weight_core.reshape(width, 3 * core_width)
    weight_out = gather(out_weight)
    weight_up = gather(up_weight)
    weight_down = gather(down_weight)

    tokens_own = arrange(inputs)
    upstream = arrange(cotangent).reshape(own_rows, width)
    tokens_theirs = flip(tokens_own, "core")
    tokens_all = join_cores(tokens_own, tokens_theirs, 2).reshape(SEG, width).astype(F32)
    tokens_own = tokens_own.reshape(own_rows, width).astype(F32)

    unit_all, _ = normalize(tokens_all)
    normed = (unit_all * gain_pre).astype(BF16)
    bias_parts = bias_qv.reshape(2, 2, core_width)
    bias_core = lax.dynamic_index_in_dim(bias_parts, core, 1, keepdims=False)
    bias_core = jnp.concatenate([bias_core[0], jnp.zeros((core_width,), F32), bias_core[1]])
    proj_t = (
        jnp.einsum("rd,df->fr", normed, weight_core, preferred_element_type=F32)
        + bias_core[:, None]
    ).astype(BF16)

    offsets = lax.dynamic_index_in_dim(
        head_offsets.reshape(2, core_heads), core, 0, keepdims=False
    )
    starts = lax.dynamic_index_in_dim(
        pic_starts.reshape(items, pic_starts.shape[2]), grp, 0, keepdims=False
    )
    starts = starts - seg * SEG
    lane = jnp.arange(SEG, dtype=jnp.int32)
    place = 2 * (lane % HALF) + lane // HALF
    inside = (place[:, None] >= starts[None, :]) & (place[:, None] < starts[None, :] + PIC)
    ends = jnp.max(jnp.where(inside, starts[None, :] + PIC - 1, -1), axis=1)
    limits = jnp.maximum(place, ends)[None, :]
    marks = 4 * TILE * jnp.arange(NT // 2, dtype=jnp.int32) + 2 * TILE
    flags = jnp.any(
        (starts[None, :] < marks[:, None]) & (starts[None, :] + PIC > marks[:, None]), axis=1
    ).astype(jnp.int32)
    far = seg.astype(jnp.int32).reshape(1)

    pair_heads = proj_t[core_width:].reshape(2, core_heads, HD, 2, HALF)
    active = (offsets == 1)[None, :, None, None]
    pair_active = jnp.where(active, pair_heads[:, :, :, 1], pair_heads[:, :, :, 0])
    pair_active = pair_active.reshape(2 * core_width, HALF)
    pair_far = lax.ppermute(pair_active, "seg", [(0, 1)])

    acc, stats = near_forward(offsets, flags, limits, proj_t)
    out_t, lse = far_forward(offsets, far, proj_t, pair_far, acc, stats)

    def split_cores(rows):
        rows = rows.reshape(2, groups, 2, half, rows.shape[-1])
        mine = lax.dynamic_index_in_dim(rows, core, 2, keepdims=False)
        other = lax.dynamic_index_in_dim(rows, 1 - core, 2, keepdims=False)
        return mine.reshape(own_rows, -1), other.reshape(own_rows, -1)

    out_mine, out_other = split_cores(out_t.T)
    out_theirs = flip(out_other, "core")
    attended = join_cores(out_mine, out_theirs, 1).reshape(own_rows, width)

    unit_mid, scale_mid = normalize(attended)
    mid_low = (unit_mid * gain_mid).astype(BF16)
    middle = tokens_own + jnp.dot(mid_low, weight_out, preferred_element_type=F32) + bias_out
    unit_ffn, scale_ffn = normalize(middle)
    ffn_low = (unit_ffn * gain_ffn).astype(BF16)
    before = jnp.dot(ffn_low, weight_up, preferred_element_type=F32) + bias_up
    activated, slope = gelu_and_slope(before)
    unit_sub, scale_sub = normalize(activated)
    sub_low = (unit_sub * gain_sub).astype(BF16)
    finished = middle + jnp.dot(sub_low, weight_down, preferred_element_type=F32) + bias_down
    layer_out = restore(finished.astype(BF16))

    def wgrad(a, b):
        return lax.dot_general(a, b, (((0,), (0,)), ((), ())), preferred_element_type=F32)

    def back(a, w):
        return lax.dot_general(a, w, (((1,), (1,)), ((), ())), preferred_element_type=F32)

    grad_downw = wgrad(sub_low, upstream)
    grad_downb = jnp.sum(upstream.astype(F32), axis=0)
    act_grad, grad_subgain = norm_back(unit_sub, scale_sub, gain_sub, back(upstream, weight_down))
    before_grad = (act_grad * slope).astype(BF16)
    grad_upw = wgrad(ffn_low, before_grad)
    grad_upb = jnp.sum(before_grad.astype(F32), axis=0)
    middle_part, grad_ffngain = norm_back(unit_ffn, scale_ffn, gain_ffn, back(before_grad, weight_up))
    middle_grad = upstream.astype(F32) + middle_part
    branch_grad = middle_grad.astype(BF16)
    grad_outw = wgrad(mid_low, branch_grad)
    grad_outb = jnp.sum(branch_grad.astype(F32), axis=0)
    attn_grad, grad_midgain = norm_back(unit_mid, scale_mid, gain_mid, back(branch_grad, weight_out))

    attn_low = attn_grad.astype(BF16).reshape(own_rows, 2, core_width)
    keep = lax.dynamic_index_in_dim(attn_low, core, 1, keepdims=False)
    give = lax.dynamic_index_in_dim(attn_low, 1 - core, 1, keepdims=False)
    take = flip(give, "core")
    shape = (2, groups, half, core_width)
    grads_all = join_cores(keep.reshape(shape), take.reshape(shape), 2)
    grads_t = grads_all.reshape(SEG, core_width).T

    dq_far, pair_back = far_backward(offsets, far, proj_t, pair_far, grads_t, out_t, lse)
    pair_recv = lax.ppermute(pair_back, "seg", [(1, 0)])
    near = near_backward(offsets, flags, limits, proj_t, grads_t, out_t, lse, dq_far)
    near_pairs = near[1:].reshape(2, core_heads, HD, 2, HALF)
    recv = pair_recv.reshape(2, core_heads, HD, 1, HALF).astype(F32)
    chosen = offsets[None, :, None, None, None] == jnp.arange(2)[None, None, None, :, None]
    pairs_t = (near_pairs.astype(F32) + jnp.where(chosen, recv, 0.0)).astype(BF16)
    proj_grad = jnp.concatenate([near[:1], pairs_t.reshape(2, core_width, SEG)], axis=0)
    proj_grad = proj_grad.reshape(3 * core_width, SEG)

    grad_core = jnp.einsum("rd,fr->df", normed, proj_grad, preferred_element_type=F32)
    sums_core = jnp.sum(proj_grad.astype(F32), axis=1).reshape(3, core_width)
    normed_part = jnp.einsum("fr,df->rd", proj_grad, weight_core, preferred_element_type=F32)
    part_mine, part_other = split_cores(normed_part)
    part_theirs = flip(part_other.astype(BF16), "core").astype(F32)
    normed_grad = part_mine + part_theirs
    unit_own, scale_own = normalize(tokens_own)
    input_part, grad_pregain = norm_back(unit_own, scale_own, gain_pre, normed_grad)
    input_grad = restore((middle_grad + input_part).astype(BF16))

    def scatter(value):
        return lax.psum_scatter(
            value.astype(BF16), ALL, scatter_dimension=0, tiled=True
        ).astype(F32)

    own_downw = scatter(grad_downw)
    own_upw = scatter(grad_upw)
    own_outw = scatter(grad_outw)
    both = lax.psum_scatter(
        grad_core.astype(BF16), ("batch", "seg", "grp"), scatter_dimension=0, tiled=True
    )
    rows = both.shape[0] // 2
    both = both.reshape(2, rows, 3, core_width)
    mine = lax.dynamic_index_in_dim(both, core, 0, keepdims=False)
    theirs = flip(lax.dynamic_index_in_dim(both, 1 - core, 0, keepdims=False), "core")
    own_qkv = join_cores(mine, theirs, 2).reshape(rows, 6 * core_width).astype(F32)

    zeros = jnp.zeros((core_width,), F32)
    on_left = core == 0
    q_sum = jnp.concatenate([jnp.where(on_left, sums_core[0], zeros), jnp.where(on_left, zeros, sums_core[0])])
    v_sum = jnp.concatenate([jnp.where(on_left, sums_core[2], zeros), jnp.where(on_left, zeros, sums_core[2])])
    grad_qvb = jnp.concatenate([q_sum, v_sum])
    vectors = (
        grad_pregain,
        grad_qvb,
        grad_midgain,
        grad_outb,
        grad_ffngain,
        grad_upb,
        grad_subgain,
        grad_downb,
    )
    devices = small_all.shape[0]
    packed = jnp.concatenate([v.reshape(devices, -1) for v in vectors], axis=1)
    packed = lax.psum_scatter(packed, ALL, scatter_dimension=0, tiled=True)[0]
    owned = []
    at = 0
    for size in sizes:
        owned.append(packed[at : at + size])
        at += size
    return (
        layer_out,
        input_grad,
        owned[0],
        own_qkv,
        owned[1],
        owned[2],
        own_outw,
        owned[3],
        owned[4],
        own_upw,
        owned[5],
        owned[6],
        own_downw,
        owned[7],
    )


def solution(mesh):
    batch = mesh.shape["batch"]
    seq = mesh.shape["seq"]
    fine = Mesh(mesh.devices.reshape(batch, 2, seq // 4, 2), ALL)
    tokens = P(None, "batch", ("seg", "grp", "core"), None)
    vector = P(ALL)
    matrix = P(ALL, None)
    return jax.shard_map(
        on_device,
        mesh=fine,
        in_specs=(
            tokens,
            tokens,
            vector,
            matrix,
            vector,
            vector,
            matrix,
            vector,
            vector,
            matrix,
            vector,
            vector,
            matrix,
            vector,
            P(None, "batch", None),
            P(),
        ),
        out_specs=(
            tokens,
            tokens,
            vector,
            matrix,
            vector,
            vector,
            matrix,
            vector,
            vector,
            matrix,
            vector,
            vector,
            matrix,
            vector,
        ),
        check_vma=False,
    )
```

```python
import math

import jax
import jax.numpy as jnp
import numpy as np
from jax import lax
from jax.experimental import pallas as pl
from jax.experimental.pallas import tpu as pltpu
from jax.sharding import Mesh
from jax.sharding import PartitionSpec as P

HEADS = 12
HD = 64
SEG = 2048
PIC = 256
HALF = SEG // 2
TILE = 512
NT = HALF // TILE
NEG = -1e30
SAFE_EXPONENT = 100.0
EXP_SCALE = math.log2(math.e) / math.sqrt(HD)
SCORE_SCALE = 1.0 / math.sqrt(HD)
ALL = ("batch", "seg", "grp", "core")
F32 = jnp.float32
BF16 = jnp.bfloat16


def dot(a, b, ca, cb):
    return lax.dot_general(a, b, (((ca,), (cb,)), ((), ())), preferred_element_type=F32)


def class_lanes(off, number, tile):
    parity = off if number == 0 else 1 - off
    return parity, pl.ds(pl.multiple_of(parity * HALF + tile * TILE, TILE), TILE)


def masked(scores, limit_row, first_key):
    keys = 2 * lax.broadcasted_iota(jnp.int32, scores.shape, 0)
    return jnp.where(keys <= limit_row - first_key, scores, NEG)


def plain_step(state, scores, values_t):
    top, total, acc = state
    weights = jnp.exp2(scores)
    total = total + jnp.sum(weights, axis=0, keepdims=True)
    acc = acc + dot(values_t, weights.astype(BF16), 1, 0)
    return (top, total, acc)


def online_step(state, scores, values_t):
    top, total, acc = state
    new_top = jnp.maximum(top, jnp.max(scores, axis=0, keepdims=True))
    factor = jnp.exp2(top - new_top)
    weights = jnp.exp2(scores - new_top)
    total = total * factor + jnp.sum(weights, axis=0, keepdims=True)
    acc = acc * factor + dot(values_t, weights.astype(BF16), 1, 0)
    return (new_top, total, acc)


def longest(values_t):
    wide = values_t.astype(F32)
    return jnp.max(jnp.sum(wide * wide, axis=0, keepdims=True))


def scores_bounded(queries_t, keys_t):
    square = longest(queries_t) * longest(keys_t) * (EXP_SCALE * EXP_SCALE)
    return square < SAFE_EXPONENT * SAFE_EXPONENT


def near_forward_kernel(off_ref, lim_ref, q_ref, k_ref, v_ref, acc_ref, stat_ref, key_ref):
    pair = pl.program_id(0)
    for h in range(2):
        for c in range(SEG // TILE):
            cols = pl.ds(c * TILE, TILE)
            key_ref[h, cols, :] = k_ref[h * HD : (h + 1) * HD, cols].T
    bounded = scores_bounded(q_ref[...], k_ref[...])

    def run(step, begin):
        def per_class(cls, carry):
            first = jnp.where(cls == 0, 1.0, 0.0).astype(F32)
            for i in range(NT):
                heads = []
                for h in range(2):
                    off = off_ref[pair * 2 + h]
                    own = jnp.where(cls == 0, off, 1 - off)
                    cols = pl.ds(pl.multiple_of(own * HALF + i * TILE, TILE), TILE)
                    heads.append((off, cols, q_ref[h * HD : (h + 1) * HD, cols], lim_ref[:, cols]))
                states = [
                    (jnp.full((1, TILE), begin, F32), jnp.zeros((1, TILE), F32), jnp.zeros((HD, TILE), F32))
                ] * 2
                for other in range(2):
                    for j in range(i + 1):
                        for h in range(2):
                            off, cols, queries, limit_row = heads[h]
                            parity, kcols = class_lanes(off, other, j)
                            scores = dot(key_ref[h, kcols, :], queries, 1, 0) * EXP_SCALE
                            if other == 0:
                                scores = scores + first
                            if j == i:
                                scores = masked(scores, limit_row, 2 * TILE * j + parity)
                            states[h] = step(states[h], scores, v_ref[h * HD : (h + 1) * HD, kcols])
                for h in range(2):
                    cols = heads[h][1]
                    top, total, acc = states[h]
                    acc_ref[h * HD : (h + 1) * HD, cols] = acc
                    stat_ref[0, h : h + 1, cols] = top
                    stat_ref[0, 2 + h : 3 + h, cols] = total
            return carry

        lax.fori_loop(0, 2, per_class, 0)

    @pl.when(bounded)
    def _():
        run(plain_step, 0.0)
        stat_ref[0, 4:5, :] = jnp.ones((1, SEG), F32)

    @pl.when(jnp.logical_not(bounded))
    def _():
        run(online_step, NEG)
        stat_ref[0, 4:5, :] = jnp.zeros((1, SEG), F32)


def far_forward_kernel(
    off_ref, far_ref, q_ref, kx_ref, vx_ref, acc_in, stat_in, ot_ref, lse_ref, o_ref, key_ref
):
    pair = pl.program_id(0)
    has_far = far_ref[0] > 0
    bounded = jnp.logical_and(
        scores_bounded(q_ref[...], kx_ref[...]), jnp.max(stat_in[0, 4:5, 0:128]) > 0.5
    )

    def finish(cols, h, state):
        rows = slice(h * HD, (h + 1) * HD)
        top, total, acc = state
        ot_ref[rows, cols] = acc / total
        lse_ref[0, h : h + 1, cols] = top + jnp.log2(total)

    def state_of(cols, h):
        return (
            stat_in[0, h : h + 1, cols],
            stat_in[0, 2 + h : 3 + h, cols],
            acc_in[h * HD : (h + 1) * HD, cols],
        )

    def run(step, width):
        for h in range(2):
            for c in range(HALF // TILE):
                cols = pl.ds(c * TILE, TILE)
                key_ref[h, cols, :] = kx_ref[h * HD : (h + 1) * HD, cols].T
        for i in range(HALF // width):
            lanes = []
            states = []
            for h in range(2):
                off = off_ref[pair * 2 + h]
                cols = pl.ds(pl.multiple_of(off * HALF + i * width, width), width)
                lanes.append(cols)
                states.append(state_of(cols, h))
            for j in range(NT):
                for h in range(2):
                    rows = slice(h * HD, (h + 1) * HD)
                    kcols = pl.ds(j * TILE, TILE)
                    scores = dot(key_ref[h, kcols, :], q_ref[rows, lanes[h]], 1, 0) * EXP_SCALE
                    states[h] = step(states[h], scores, vx_ref[rows, kcols])
            for h in range(2):
                finish(lanes[h], h, states[h])

    @pl.when(jnp.logical_and(has_far, bounded))
    def _():
        run(plain_step, HALF)

    @pl.when(jnp.logical_and(has_far, jnp.logical_not(bounded)))
    def _():
        run(online_step, TILE)

    @pl.when(jnp.logical_not(has_far))
    def _():
        for h in range(2):
            cols = pl.ds(pl.multiple_of(off_ref[pair * 2 + h] * HALF, HALF), HALF)
            finish(cols, h, state_of(cols, h))

    for h in range(2):
        cols = pl.ds(pl.multiple_of((1 - off_ref[pair * 2 + h]) * HALF, HALF), HALF)
        finish(cols, h, state_of(cols, h))
    for c in range(SEG // TILE):
        cols = pl.ds(c * TILE, TILE)
        o_ref[cols, :] = ot_ref[:, cols].T


def slopes_of(scores, lse_row, inner, dot_row):
    probs = jnp.exp2(scores - lse_row)
    return probs.astype(BF16), (probs * (inner - dot_row)).astype(BF16)


def far_backward_kernel(
    off_ref,
    far_ref,
    q_ref,
    kx_ref,
    vx_ref,
    g_ref,
    ot_ref,
    lse_ref,
    dq_ref,
    dkv_ref,
    key_ref,
    val_ref,
    gt_ref,
    acc_ref,
):
    pair = pl.program_id(0)

    @pl.when(far_ref[0] == 0)
    def _():
        dq_ref[...] = jnp.zeros_like(dq_ref)
        dkv_ref[...] = jnp.zeros_like(dkv_ref)

    @pl.when(far_ref[0] > 0)
    def _():
        for c in range(SEG // TILE):
            gt_ref[:, pl.ds(c * TILE, TILE)] = g_ref[pl.ds(c * TILE, TILE), :].T
        for h in range(2):
            rows = slice(h * HD, (h + 1) * HD)
            for c in range(HALF // TILE):
                cols = pl.ds(c * TILE, TILE)
                key_ref[h, cols, :] = kx_ref[rows, cols].T
                val_ref[h, cols, :] = vx_ref[rows, cols].T
        for h in range(2):
            rows = slice(h * HD, (h + 1) * HD)
            off = off_ref[pair * 2 + h]
            qcols = pl.ds(pl.multiple_of(off * HALF, HALF), HALF)
            queries = q_ref[rows, qcols]
            grads = gt_ref[rows, qcols]
            lse_row = lse_ref[0, h : h + 1, qcols]
            dot_row = jnp.sum(grads.astype(F32) * ot_ref[rows, qcols], axis=0, keepdims=True)
            total = jnp.zeros((HD, HALF), F32)
            for j in range(NT):
                kcols = pl.ds(j * TILE, TILE)
                scores = dot(key_ref[h, kcols, :], queries, 1, 0) * EXP_SCALE
                inner = dot(val_ref[h, kcols, :], grads, 1, 0)
                probs, slopes = slopes_of(scores, lse_row, inner, dot_row)
                acc_ref[rows, kcols] = (dot(queries, slopes, 1, 1) * SCORE_SCALE).astype(BF16)
                acc_ref[2 * HD + h * HD : 2 * HD + (h + 1) * HD, kcols] = dot(grads, probs, 1, 1).astype(BF16)
                total = total + dot(kx_ref[rows, kcols], slopes, 1, 0)
            dq_ref[rows, :] = total
        for c in range(HALF // TILE):
            cols = pl.ds(c * TILE, TILE)
            dkv_ref[0, cols, :] = acc_ref[: 2 * HD, cols].T
            dkv_ref[1, cols, :] = acc_ref[2 * HD :, cols].T


def near_backward_kernel(
    off_ref,
    lim_ref,
    q_ref,
    k_ref,
    v_ref,
    g_ref,
    ot_ref,
    lse_ref,
    dqx_ref,
    out_q_ref,
    out_ref,
    key_ref,
    val_ref,
    gt_ref,
    dq_ref,
    row_ref,
    acc_ref,
):
    pair = pl.program_id(0)
    for c in range(SEG // TILE):
        gt_ref[:, pl.ds(c * TILE, TILE)] = g_ref[pl.ds(c * TILE, TILE), :].T
    for h in range(2):
        rows = slice(h * HD, (h + 1) * HD)
        off = off_ref[pair * 2 + h]
        for c in range(SEG // TILE):
            cols = pl.ds(c * TILE, TILE)
            key_ref[h, cols, :] = k_ref[rows, cols].T
            val_ref[h, cols, :] = v_ref[rows, cols].T
            row_ref[h : h + 1, cols] = jnp.sum(
                gt_ref[rows, cols].astype(F32) * ot_ref[rows, cols], axis=0, keepdims=True
            )
        active = pl.ds(pl.multiple_of(off * HALF, HALF), HALF)
        rest = pl.ds(pl.multiple_of((1 - off) * HALF, HALF), HALF)
        dq_ref[rows, active] = dqx_ref[rows, :]
        dq_ref[rows, rest] = jnp.zeros((HD, HALF), F32)

    def per_class(cls, carry):
        first = jnp.where(cls == 0, 1.0, 0.0).astype(F32)
        for j in range(NT):
            lanes = []
            for h in range(2):
                off = off_ref[pair * 2 + h]
                parity = jnp.where(cls == 0, off, 1 - off)
                lanes.append((parity, pl.ds(pl.multiple_of(parity * HALF + j * TILE, TILE), TILE)))
            sums = [(jnp.zeros((HD, TILE), F32), jnp.zeros((HD, TILE), F32))] * 2
            for other in range(2):
                for i in range(j, NT):
                    for h in range(2):
                        rows = slice(h * HD, (h + 1) * HD)
                        parity, kcols = lanes[h]
                        _, qcols = class_lanes(off_ref[pair * 2 + h], other, i)
                        queries = q_ref[rows, qcols]
                        grads = gt_ref[rows, qcols]
                        lse_row = lse_ref[0, h : h + 1, qcols]
                        if other == 0:
                            lse_row = lse_row - first
                        scores = dot(key_ref[h, kcols, :], queries, 1, 0) * EXP_SCALE
                        if i == j:
                            scores = masked(scores, lim_ref[:, qcols], 2 * TILE * j + parity)
                        inner = dot(val_ref[h, kcols, :], grads, 1, 0)
                        probs, slopes = slopes_of(scores, lse_row, inner, row_ref[h : h + 1, qcols])
                        dk, dv = sums[h]
                        sums[h] = (dk + dot(queries, slopes, 1, 1), dv + dot(grads, probs, 1, 1))
                        dq_ref[rows, qcols] += dot(k_ref[rows, kcols], slopes, 1, 0)
            for h in range(2):
                rows = slice(h * HD, (h + 1) * HD)
                kcols = lanes[h][1]
                acc_ref[rows, kcols] = (sums[h][0] * SCORE_SCALE).astype(BF16)
                acc_ref[2 * HD + h * HD : 2 * HD + (h + 1) * HD, kcols] = sums[h][1].astype(BF16)
        return carry

    lax.fori_loop(0, 2, per_class, 0)
    for c in range(SEG // TILE):
        cols = pl.ds(c * TILE, TILE)
        out_q_ref[cols, :] = (dq_ref[:, cols] * SCORE_SCALE).astype(BF16).T
        out_ref[0, cols, :] = acc_ref[: 2 * HD, cols].T
        out_ref[1, cols, :] = acc_ref[2 * HD :, cols].T


def smem():
    return pl.BlockSpec(memory_space=pltpu.SMEM)


def rows_spec(first, width=SEG):
    return pl.BlockSpec((2 * HD, width), lambda p, f=first: (f + p, 0))


def cols_spec():
    return pl.BlockSpec((SEG, 2 * HD), lambda p: (0, p))


def stat_spec():
    return pl.BlockSpec((1, 8, SEG), lambda p: (p, 0, 0))


def limit_spec():
    return pl.BlockSpec((1, SEG), lambda p: (0, 0))


def cost(pairs, matmuls, scores, size):
    return pl.CostEstimate(
        flops=pairs * 2 * matmuls * 2 * HD * scores, transcendentals=pairs * 2 * scores, bytes_accessed=size
    )


def near_forward(offsets, limits, proj_t):
    pairs = offsets.shape[0] // 2
    return pl.pallas_call(
        near_forward_kernel,
        grid=(pairs,),
        in_specs=[smem(), limit_spec(), rows_spec(0), rows_spec(pairs), rows_spec(2 * pairs)],
        out_specs=[rows_spec(0), stat_spec()],
        out_shape=[
            jax.ShapeDtypeStruct((pairs * 2 * HD, SEG), F32),
            jax.ShapeDtypeStruct((pairs, 8, SEG), F32),
        ],
        scratch_shapes=[pltpu.VMEM((2, SEG, HD), BF16)],
        cost_estimate=cost(pairs, 8, 3 * HALF * HALF, 8 << 20),
        name="near_forward",
    )(offsets, limits, proj_t, proj_t, proj_t)


def far_forward(offsets, far, proj_t, pair_t, acc, stats):
    pairs = offsets.shape[0] // 2
    return pl.pallas_call(
        far_forward_kernel,
        grid=(pairs,),
        in_specs=[
            smem(),
            smem(),
            rows_spec(0),
            rows_spec(0, HALF),
            rows_spec(pairs, HALF),
            rows_spec(0),
            stat_spec(),
        ],
        out_specs=[rows_spec(0), stat_spec(), cols_spec()],
        out_shape=[
            jax.ShapeDtypeStruct((pairs * 2 * HD, SEG), F32),
            jax.ShapeDtypeStruct((pairs, 8, SEG), F32),
            jax.ShapeDtypeStruct((SEG, pairs * 2 * HD), F32),
        ],
        scratch_shapes=[pltpu.VMEM((2, HALF, HD), BF16)],
        cost_estimate=cost(pairs, 8, HALF * HALF, 12 << 20),
        name="far_forward",
    )(offsets, far, proj_t, pair_t, pair_t, acc, stats)


def far_backward(offsets, far, proj_t, pair_t, grads, out_t, lse):
    pairs = offsets.shape[0] // 2
    return pl.pallas_call(
        far_backward_kernel,
        grid=(pairs,),
        in_specs=[
            smem(),
            smem(),
            rows_spec(0),
            rows_spec(0, HALF),
            rows_spec(pairs, HALF),
            cols_spec(),
            rows_spec(0),
            stat_spec(),
        ],
        out_specs=[
            rows_spec(0, HALF),
            pl.BlockSpec((2, HALF, 2 * HD), lambda p: (0, 0, p)),
        ],
        out_shape=[
            jax.ShapeDtypeStruct((pairs * 2 * HD, HALF), F32),
            jax.ShapeDtypeStruct((2, HALF, pairs * 2 * HD), BF16),
        ],
        scratch_shapes=[
            pltpu.VMEM((2, HALF, HD), BF16),
            pltpu.VMEM((2, HALF, HD), BF16),
            pltpu.VMEM((2 * HD, SEG), BF16),
            pltpu.VMEM((4 * HD, HALF), BF16),
        ],
        cost_estimate=cost(pairs, 20, HALF * HALF, 10 << 20),
        name="far_backward",
    )(offsets, far, proj_t, pair_t, pair_t, grads, out_t, lse)


def near_backward(offsets, limits, proj_t, grads, out_t, lse, dq_far):
    pairs = offsets.shape[0] // 2
    return pl.pallas_call(
        near_backward_kernel,
        grid=(pairs,),
        in_specs=[
            smem(),
            limit_spec(),
            rows_spec(0),
            rows_spec(pairs),
            rows_spec(2 * pairs),
            cols_spec(),
            rows_spec(0),
            stat_spec(),
            rows_spec(0, HALF),
        ],
        out_specs=[cols_spec(), pl.BlockSpec((2, SEG, 2 * HD), lambda p: (0, 0, p))],
        out_shape=[
            jax.ShapeDtypeStruct((SEG, pairs * 2 * HD), BF16),
            jax.ShapeDtypeStruct((2, SEG, pairs * 2 * HD), BF16),
        ],
        scratch_shapes=[
            pltpu.VMEM((2, SEG, HD), BF16),
            pltpu.VMEM((2, SEG, HD), BF16),
            pltpu.VMEM((2 * HD, SEG), BF16),
            pltpu.VMEM((2 * HD, SEG), F32),
            pltpu.VMEM((8, SEG), F32),
            pltpu.VMEM((4 * HD, SEG), BF16),
        ],
        cost_estimate=cost(pairs, 20, 3 * HALF * HALF, 14 << 20),
        name="near_backward",
    )(offsets, limits, proj_t, proj_t, proj_t, grads, out_t, lse, dq_far)


def normalize(values):
    centred = values - jnp.mean(values, axis=-1, keepdims=True)
    spread = jnp.mean(centred * centred, axis=-1, keepdims=True)
    scale = lax.rsqrt(spread + 1e-05)
    return centred * scale, scale


def norm_back(unit, scale, gain, grad):
    scaled = grad * gain
    first = jnp.mean(scaled, axis=-1, keepdims=True)
    second = jnp.mean(scaled * unit, axis=-1, keepdims=True)
    values = (scaled - first - unit * second) * scale
    return values, jnp.sum(grad * unit, axis=0)


def gelu_and_slope(u):
    cdf = 0.5 * (1.0 + lax.erf(u * math.sqrt(0.5)))
    density = jnp.exp(-0.5 * u * u) * (1.0 / math.sqrt(2.0 * math.pi))
    return u * cdf, cdf + u * density


def flip(values, axis):
    return lax.ppermute(values, axis, [(0, 1), (1, 0)])


def spread_items(items):
    groups = lax.axis_size("grp")
    if groups != 2:
        return lax.all_to_all(items, "grp", 0, 0, tiled=True)
    me = lax.axis_index("grp")
    mine = lax.dynamic_index_in_dim(items, me, 0, keepdims=False)
    other = flip(lax.dynamic_index_in_dim(items, 1 - me, 0, keepdims=False), "grp")
    swap = me == 1
    return jnp.stack([jnp.where(swap, other, mine), jnp.where(swap, mine, other)])


def shifted(values, amount):
    count = lax.axis_size("batch")
    return lax.ppermute(values, "batch", [(i, (i + amount) % count) for i in range(count)])


def across(values, ds, dg):
    table = [(2 * s + g, 2 * (s ^ ds) + (g ^ dg)) for s in range(2) for g in range(2)]
    return lax.ppermute(values, ("seg", "grp"), table)


OTHERS = ((1, 0), (0, 1), (1, 1))


def together(*values):
    return lax.optimization_barrier(values)


def column_pieces(shard):
    return [shifted(shard, k) for k in range(1, lax.axis_size("batch"))]


def column_place(own, pieces):
    count = lax.axis_size("batch")
    batch = lax.axis_index("batch")
    column = jnp.zeros((count,) + own.shape, own.dtype)
    for k, piece in enumerate([own] + list(pieces)):
        column = lax.dynamic_update_index_in_dim(column, piece, (batch + count - k) % count, 0)
    return column


def plane_pieces(values):
    return [across(values, ds, dg) for ds, dg in OTHERS]


def plane_place(own, pieces):
    seg, grp = lax.axis_index("seg"), lax.axis_index("grp")
    plane = jnp.zeros((2, 2) + own.shape, own.dtype)
    zero = jnp.zeros((), jnp.int32)
    for (ds, dg), piece in zip(((0, 0),) + OTHERS, [own] + list(pieces)):
        place = (seg ^ ds, grp ^ dg) + (zero,) * own.ndim
        plane = lax.dynamic_update_slice(plane, piece[None, None], place)
    return plane


def plane_part(parts, ds, dg):
    seg, grp = lax.axis_index("seg"), lax.axis_index("grp")
    rows = lax.dynamic_index_in_dim(parts, seg ^ ds, 0, keepdims=False)
    return lax.dynamic_index_in_dim(rows, grp ^ dg, 0, keepdims=False)


def plane_sends(parts):
    return [across(plane_part(parts, ds, dg), ds, dg) for ds, dg in OTHERS]


def plane_sum(parts, received):
    total = plane_part(parts, 0, 0).astype(F32)
    for piece in received:
        total = total + piece.astype(F32)
    return total


def column_sends(column):
    count = lax.axis_size("batch")
    batch = lax.axis_index("batch")
    low = column.astype(BF16)
    return [
        shifted(lax.dynamic_index_in_dim(low, (batch + k) % count, 0, keepdims=False), k)
        for k in range(1, count)
    ]


def column_sum(column, received):
    total = lax.dynamic_index_in_dim(column, lax.axis_index("batch"), 0, keepdims=False)
    for piece in received:
        total = total + piece.astype(F32)
    return total


def on_device(
    inputs,
    cotangent,
    pre_gain,
    qkv_weight,
    qv_bias,
    mid_gain,
    out_weight,
    out_bias,
    ffn_gain,
    up_weight,
    up_bias,
    sub_gain,
    down_weight,
    down_bias,
    pic_starts,
    head_offsets,
):
    micro, sequences, local, width = inputs.shape
    groups = lax.axis_size("grp")
    items = micro * sequences
    half = local // 2
    own_rows = groups * local
    core_heads = HEADS // 2
    core_width = core_heads * HD
    batches = lax.axis_size("batch")
    seg = lax.axis_index("seg")
    grp = lax.axis_index("grp")
    core = lax.axis_index("core")
    staged = groups == 2

    order = np.concatenate([np.arange(0, local, 2), np.arange(1, local, 2)])
    split = np.zeros((local, local), np.float32)
    split[np.arange(local), order] = 1.0
    split = jnp.asarray(split, BF16)

    def arrange(tokens):
        tokens = spread_items(tokens.reshape(items, local, width))
        tokens = jnp.einsum("rs,isd->ird", split, tokens, preferred_element_type=F32).astype(BF16)
        return tokens.reshape(groups, 2, half, width).transpose(1, 0, 2, 3)

    def restore(tokens):
        tokens = tokens.reshape(2, groups, half, width).transpose(1, 0, 2, 3)
        tokens = spread_items(tokens.reshape(groups, local, width))
        tokens = jnp.einsum("rs,ird->isd", split, tokens, preferred_element_type=F32).astype(BF16)
        return tokens.reshape(inputs.shape)

    def join_cores(own, theirs, axis):
        swap = core == 1
        return jnp.stack([jnp.where(swap, theirs, own), jnp.where(swap, own, theirs)], axis=axis)

    rows = qkv_weight.shape[0]
    ff = up_weight.shape[1]
    cut = width // 2

    def column_halves(value):
        size = value.shape[1] // 2
        return [lax.dynamic_slice_in_dim(value, i * size, size, 1) for i in (core, 1 - core)]

    def core_rows(values):
        halves = [column_halves(value) for value in values]
        mine, other = (jnp.concatenate([half[i] for half in halves], axis=1) for i in range(2))
        both = join_cores(mine, flip(other, "core"), 0)
        return both.reshape(-1, both.shape[2])

    def whole_columns(own, other):
        swap = core == 1
        return jnp.concatenate([jnp.where(swap, other, own), jnp.where(swap, own, other)], axis=1)

    def library_gather(shard):
        whole = lax.all_gather(shard, ("batch", "seg", "grp"), axis=0)
        return whole.reshape(-1, shard.shape[1])

    tokens_own = spread_items(inputs.reshape(items, local, width))

    vectors = (pre_gain, qv_bias, mid_gain, out_bias, ffn_gain, up_bias, sub_gain, down_bias)
    counts = [v.shape[0] // rows for v in vectors]
    small = jnp.concatenate([v.reshape(rows, -1) for v in vectors], axis=1)
    small = jnp.pad(small, ((0, 0), (0, 128 - small.shape[1])))
    halves = qkv_weight.reshape(rows, 3, 2, core_width)
    mine = lax.dynamic_index_in_dim(halves, core, 2, keepdims=False)
    other = lax.dynamic_index_in_dim(halves, 1 - core, 2, keepdims=False)
    mine = jnp.concatenate([mine.reshape(rows, -1), small], axis=1)
    other = jnp.concatenate([other.reshape(rows, -1), small], axis=1)
    first = join_cores(mine, flip(other, "core"), 0).reshape(2 * rows, -1)
    wide = core_rows([out_weight, up_weight])
    deep = core_rows([down_weight])

    if staged:
        column = column_place(first, column_pieces(first))
        wide_plane = plane_place(wide, plane_pieces(wide))
        wide_plane, deep_shard, column = together(wide_plane, deep, column)
        wide_pieces = column_pieces(wide_plane)
        deep_pieces = column_pieces(deep_shard)
        first = plane_place(column, plane_pieces(column))
        first = first.transpose(2, 0, 1, 3, 4).reshape(width, -1)
    else:
        first = library_gather(first)

    tokens_own = jnp.einsum("rs,isd->ird", split, tokens_own, preferred_element_type=F32).astype(BF16)
    tokens_own = tokens_own.reshape(groups, 2, half, width).transpose(1, 0, 2, 3)
    tokens_theirs = flip(tokens_own, "core")
    tokens_all = join_cores(tokens_own, tokens_theirs, 2).reshape(SEG, width).astype(F32)
    tokens_own = tokens_own.reshape(own_rows, width).astype(F32)
    unit_all, _ = normalize(tokens_all)

    if staged:
        first, unit_all, wide_pieces[0], wide_pieces[-1] = together(
            first, unit_all, wide_pieces[0], wide_pieces[-1]
        )
    weight_core = first[:, : 3 * core_width]
    small_all = first[:, 3 * core_width :].astype(F32)
    parts = []
    at = 0
    for count in counts:
        parts.append(small_all[:, at : at + count].reshape(-1))
        at += count
    gain_pre, bias_qv, gain_mid, bias_out, gain_ffn, bias_up, gain_sub, bias_down = parts
    normed = (unit_all * gain_pre).astype(BF16)
    bias_parts = bias_qv.reshape(2, 2, core_width)
    bias_core = lax.dynamic_index_in_dim(bias_parts, core, 1, keepdims=False)
    bias_core = jnp.concatenate([bias_core[0], jnp.zeros((core_width,), F32), bias_core[1]])
    proj_t = (
        jnp.einsum("rd,df->fr", normed, weight_core, preferred_element_type=F32)
        + bias_core[:, None]
    ).astype(BF16)

    offsets = lax.dynamic_index_in_dim(
        head_offsets.reshape(2, core_heads), core, 0, keepdims=False
    )
    starts = lax.dynamic_index_in_dim(
        pic_starts.reshape(items, pic_starts.shape[2]), grp, 0, keepdims=False
    )
    starts = starts - seg * SEG
    lane = jnp.arange(SEG, dtype=jnp.int32)
    place = 2 * (lane % HALF) + lane // HALF
    inside = (place[:, None] >= starts[None, :]) & (place[:, None] < starts[None, :] + PIC)
    ends = jnp.max(jnp.where(inside, starts[None, :] + PIC - 1, -1), axis=1)
    limits = jnp.maximum(place, ends)[None, :]
    far = seg.astype(jnp.int32).reshape(1)

    odd_rows = jnp.tile(jnp.repeat(offsets, HD), 2) == 1
    pairs_all = proj_t[core_width:]
    pair_active = jnp.where(odd_rows[:, None], pairs_all[:, HALF:], pairs_all[:, :HALF])
    pair_far = lax.ppermute(pair_active, "seg", [(0, 1)])

    acc, stats = near_forward(offsets, limits, proj_t)
    if staged:
        cotangent, acc, stats, pair_far, deep_pieces, wide_pieces = together(
            cotangent, acc, stats, pair_far, deep_pieces, wide_pieces
        )
        wide_own = column_place(wide_plane, wide_pieces).reshape(width, -1)
        deep_column = column_place(deep, deep_pieces)
        deep_planes = plane_pieces(deep_column)
    else:
        wide_own = library_gather(wide)
        deep_own = library_gather(deep)
    wide_other = flip(wide_own, "core")
    upstream = arrange(cotangent).reshape(own_rows, width)
    out_t, lse, out_rows = far_forward(offsets, far, proj_t, pair_far, acc, stats)

    def split_cores(rows):
        rows = rows.reshape(2, groups, 2, half, rows.shape[-1])
        mine = lax.dynamic_index_in_dim(rows, core, 2, keepdims=False)
        other = lax.dynamic_index_in_dim(rows, 1 - core, 2, keepdims=False)
        return mine.reshape(own_rows, -1), other.reshape(own_rows, -1)

    out_mine, out_other = split_cores(out_rows)
    out_theirs = flip(out_other, "core")
    attended = join_cores(out_mine, out_theirs, 1).reshape(own_rows, width)
    weight_out = whole_columns(wide_own[:, :cut], wide_other[:, :cut])
    weight_up = whole_columns(wide_own[:, cut:], wide_other[:, cut:])

    unit_mid, scale_mid = normalize(attended)
    mid_low = (unit_mid * gain_mid).astype(BF16)
    middle = tokens_own + jnp.dot(mid_low, weight_out, preferred_element_type=F32) + bias_out
    unit_ffn, scale_ffn = normalize(middle)
    ffn_low = (unit_ffn * gain_ffn).astype(BF16)
    before = jnp.dot(ffn_low, weight_up, preferred_element_type=F32) + bias_up
    if staged:
        before, upstream, deep_planes = together(before, upstream, deep_planes)
        deep_own = plane_place(deep_column, deep_planes)
        deep_own = deep_own.transpose(2, 0, 1, 3, 4).reshape(ff, -1)
    deep_other = flip(deep_own, "core")
    weight_down = whole_columns(deep_own, deep_other)
    activated, slope = gelu_and_slope(before)
    unit_sub, scale_sub = normalize(activated)
    sub_low = (unit_sub * gain_sub).astype(BF16)
    finished = middle + jnp.dot(sub_low, weight_down, preferred_element_type=F32) + bias_down
    layer_out = restore(finished.astype(BF16))

    def wgrad(a, b):
        return lax.dot_general(a, b, (((0,), (0,)), ((), ())), preferred_element_type=F32)

    def back(a, w):
        return lax.dot_general(a, w, (((1,), (1,)), ((), ())), preferred_element_type=F32)

    grad_downw = wgrad(sub_low, upstream)
    grad_downb = jnp.sum(upstream.astype(F32), axis=0)
    act_grad, grad_subgain = norm_back(unit_sub, scale_sub, gain_sub, back(upstream, weight_down))
    before_grad = (act_grad * slope).astype(BF16)
    grad_upw = wgrad(ffn_low, before_grad)
    grad_upb = jnp.sum(before_grad.astype(F32), axis=0)
    middle_part, grad_ffngain = norm_back(unit_ffn, scale_ffn, gain_ffn, back(before_grad, weight_up))
    middle_grad = upstream.astype(F32) + middle_part
    branch_grad = middle_grad.astype(BF16)
    grad_outw = wgrad(mid_low, branch_grad)
    grad_outb = jnp.sum(branch_grad.astype(F32), axis=0)
    attn_grad, grad_midgain = norm_back(unit_mid, scale_mid, gain_mid, back(branch_grad, weight_out))

    def core_sum(values):
        halves = [column_halves(value.astype(BF16)) for value in values]
        mine, other = (jnp.concatenate([half[i] for half in halves], axis=1) for i in range(2))
        summed = (mine.astype(F32) + flip(other, "core").astype(F32)).astype(BF16)
        per_chip = summed.shape[0] // (batches * 2 * groups)
        return summed.reshape(batches, 2, groups, per_chip, -1).transpose(1, 2, 0, 3, 4)

    def library_scatter(parts):
        flat = parts.transpose(2, 0, 1, 3, 4).reshape((-1,) + parts.shape[3:])
        return lax.psum_scatter(flat, ("batch", "seg", "grp"), scatter_dimension=0).astype(F32)

    attn_low = attn_grad.astype(BF16).reshape(own_rows, 2, core_width)
    keep = lax.dynamic_index_in_dim(attn_low, core, 1, keepdims=False)
    give = lax.dynamic_index_in_dim(attn_low, 1 - core, 1, keepdims=False)
    take = flip(give, "core")
    deep_parts = core_sum([grad_downw])
    wide_parts = core_sum([grad_outw, grad_upw])
    if staged:
        take, deep_parts, wide_parts = together(take, deep_parts, wide_parts)
        deep_received = plane_sends(deep_parts)
        wide_received = plane_sends(wide_parts)
    shape = (2, groups, half, core_width)
    grads_all = join_cores(keep.reshape(shape), take.reshape(shape), 2)
    grads_rows = grads_all.reshape(SEG, core_width)

    dq_far, pair_back = far_backward(offsets, far, proj_t, pair_far, grads_rows, out_t, lse)
    pair_recv = lax.ppermute(pair_back, "seg", [(1, 0)])
    if staged:
        dq_far, deep_received = together(dq_far, deep_received)
        deep_column = plane_sum(deep_parts, deep_received)
        deep_sends = column_sends(deep_column)
    grad_q, grad_near = near_backward(offsets, limits, proj_t, grads_rows, out_t, lse, dq_far)
    if staged:
        grad_q, grad_near, pair_recv, deep_sends, wide_received = together(
            grad_q, grad_near, pair_recv, deep_sends, wide_received
        )
        deep_total = column_sum(deep_column, deep_sends)
        wide_column = plane_sum(wide_parts, wide_received)
        wide_total = column_sum(wide_column, column_sends(wide_column))
    else:
        deep_total = library_scatter(deep_parts)
        wide_total = library_scatter(wide_parts)
    parity = lax.broadcasted_iota(jnp.int32, (1, 2, 1, 1), 1)
    chosen = jnp.repeat(offsets, HD)[None, None, None, :] == parity
    grad_pair = grad_near.reshape(2, 2, HALF, core_width).astype(F32)
    grad_pair = grad_pair + jnp.where(chosen, pair_recv[:, None].astype(F32), 0.0)
    grad_pair = grad_pair.astype(BF16).reshape(2, SEG, core_width)
    proj_grads = (grad_q, grad_pair[0], grad_pair[1])
    weight_cols = [weight_core[:, i * core_width : (i + 1) * core_width] for i in range(3)]
    grad_core = jnp.concatenate([wgrad(normed, g).astype(BF16) for g in proj_grads], axis=1)
    sums_core = [jnp.sum(g.astype(F32), axis=0) for g in proj_grads]
    normed_part = back(proj_grads[0], weight_cols[0])
    normed_part = normed_part + back(proj_grads[1], weight_cols[1]) + back(proj_grads[2], weight_cols[2])
    part_mine, part_other = split_cores(normed_part)
    part_theirs = flip(part_other.astype(BF16), "core").astype(F32)
    normed_grad = part_mine + part_theirs
    unit_own, scale_own = normalize(tokens_own)
    input_part, grad_pregain = norm_back(unit_own, scale_own, gain_pre, normed_grad)
    input_grad = restore((middle_grad + input_part).astype(BF16))

    def finish_halves(total, cuts):
        total = total.reshape(2, total.shape[0] // 2, -1)
        mine = lax.dynamic_index_in_dim(total, core, 0, keepdims=False)
        theirs = lax.dynamic_index_in_dim(total, 1 - core, 0, keepdims=False)
        theirs = flip(theirs.astype(BF16), "core").astype(F32)
        out = []
        at = 0
        for cut in cuts:
            out.append(whole_columns(mine[:, at : at + cut], theirs[:, at : at + cut]))
            at += cut
        return out

    own_outw, own_upw = finish_halves(wide_total, [cut, ff // 2])
    own_downw = finish_halves(deep_total, [cut])[0]

    zeros = jnp.zeros((core_width,), F32)
    on_left = core == 0
    q_sum = jnp.concatenate([jnp.where(on_left, sums_core[0], zeros), jnp.where(on_left, zeros, sums_core[0])])
    v_sum = jnp.concatenate([jnp.where(on_left, sums_core[2], zeros), jnp.where(on_left, zeros, sums_core[2])])
    grad_qvb = jnp.concatenate([q_sum, v_sum])
    vector_grads = (
        grad_pregain,
        grad_qvb,
        grad_midgain,
        grad_outb,
        grad_ffngain,
        grad_upb,
        grad_subgain,
        grad_downb,
    )
    packed = jnp.concatenate([v.reshape(width, -1) for v in vector_grads], axis=1)
    packed = jnp.pad(packed, ((0, 0), (0, 128 - packed.shape[1])))
    tail = jnp.concatenate([grad_core, packed.astype(BF16)], axis=1)
    tail = tail.reshape(batches, 2, groups, 2 * rows, -1).transpose(1, 2, 0, 3, 4)
    if staged:
        tail_column = plane_sum(tail, plane_sends(tail))
        tail = column_sum(tail_column, column_sends(tail_column))
    else:
        tail = library_scatter(tail)
    tail = tail.reshape(2, rows, -1)
    mine = lax.dynamic_index_in_dim(tail, core, 0, keepdims=False)
    theirs = lax.dynamic_index_in_dim(tail, 1 - core, 0, keepdims=False)
    theirs = flip(theirs.astype(BF16), "core").astype(F32)
    columns = 3 * core_width
    own_qkv = join_cores(
        mine[:, :columns].reshape(rows, 3, core_width), theirs[:, :columns].reshape(rows, 3, core_width), 2
    ).reshape(rows, 2 * columns)
    own_small = mine[:, columns:] + theirs[:, columns:]
    owned = []
    at = 0
    for count in counts:
        owned.append(own_small[:, at : at + count].reshape(-1))
        at += count
    return (
        layer_out,
        input_grad,
        owned[0],
        own_qkv,
        owned[1],
        owned[2],
        own_outw,
        owned[3],
        owned[4],
        own_upw,
        owned[5],
        owned[6],
        own_downw,
        owned[7],
    )


def solution(mesh):
    batch = mesh.shape["batch"]
    seq = mesh.shape["seq"]
    fine = Mesh(mesh.devices.reshape(batch, 2, seq // 4, 2), ALL)
    tokens = P(None, "batch", ("seg", "grp", "core"), None)
    vector = P(ALL)
    matrix = P(ALL, None)
    return jax.shard_map(
        on_device,
        mesh=fine,
        in_specs=(
            tokens,
            tokens,
            vector,
            matrix,
            vector,
            vector,
            matrix,
            vector,
            vector,
            matrix,
            vector,
            vector,
            matrix,
            vector,
            P(None, "batch", None),
            P(),
        ),
        out_specs=(
            tokens,
            tokens,
            vector,
            matrix,
            vector,
            vector,
            matrix,
            vector,
            vector,
            matrix,
            vector,
            vector,
            matrix,
            vector,
        ),
        check_vma=False,
    )
```
